32 devices in a mesh: gx: 8 (over y, x, core), gy: 4 (over z).
Axes of the slice: x: 2, y: 2, z: 4, core: 2. Of those that a mesh axis runs over, the one named last changes fastest.
Arguments:
- blocks: bfloat16 [8, 4, 128, 128, 128], P('gx', 'gy'), may hold values from -0.1875 to 0.1875
- pattern: int32 [8, 4, 128], P('gx', 'gy'), may hold values from 0 to 255, as said below
- local_src: bfloat16 [8, 4, 2, 32, 2048], P('gx', 'gy'), may hold values from -4 to 4
- owner: int32 [2, 32], replicated, may hold values from 0 to 31
Outputs:
- sweep_out: bfloat16 [8, 4, 2, 32, 2048], P('gx', 'gy')
The draws below stay inside these ranges and needn't reach their ends.
Inputs may be any that keep to these rules, and one draw needn't show every extreme that they name: `pattern`: the 128 values of one cell are distinct.
All inputs are finite; a program needn't handle non-finite values.
Results may differ from the reference program's by a relative error of at most 0.019.
Values may be sent and summed in bfloat16 or wider, within the bound.
A program may use at most 64 MiB of HBM per device.

```python
import jax
import jax.numpy as jnp
from jax import lax

TR = 1024
BS = 128
NBLK = 16
NNZ = 128
S = 32
NB = 2
NX = 8
NY = 4


def draw_pattern(key, part):
    keys = jax.random.split(key, NX * NY)
    perms = jax.vmap(lambda one_key: jax.random.permutation(one_key, NBLK * NBLK))(keys)
    return perms[:, :NNZ].reshape(NX, NY, NNZ).astype(jnp.int32)


def set_ends(values, stream_key, smallest, high):
    longest = values.shape.index(max(values.shape))
    spots = []
    for shift in (0, 1):
        where = [jax.random.randint(jax.random.fold_in(stream_key, axis), (), 0, length) for axis, length in enumerate(values.shape)]
        where[longest] = (where[longest] + shift) % values.shape[longest]
        spots.append(tuple(where))
    return values.at[spots[0]].set(smallest).at[spots[1]].set(high)


def block_scale(own_key, dims, cuts, low, high):
    factor_of = 1.0
    for dim, parts in cuts:
        steps = jax.random.uniform(jax.random.fold_in(jax.random.fold_in(own_key, 6), dim), (parts,), jnp.float32, low / len(cuts), high / len(cuts))
        factor_of = factor_of * jnp.repeat(jnp.exp(steps), dims[dim] // parts).reshape((-1,) + (1,) * (len(dims) - 1 - dim))
    return factor_of


def centred(rng, dims, spread, limit, pieces=(), kind=jnp.bfloat16):
    gain = block_scale(rng, dims, pieces, -0.22, 0.18) if pieces else 1.0
    drawn = jax.random.normal(rng, dims, jnp.float32) * spread * gain
    return jnp.minimum(jnp.maximum(drawn, -limit), limit).astype(kind)


def setup_inputs(seed: int = 0) -> dict:
    key_of = jax.random.split(jax.random.key(seed), 5)
    return {
        "blocks": centred(key_of[0], (NX, NY, NNZ, BS, BS), (NNZ * BS * BS // (2 * TR)) ** -0.5, 0.1875, ((0, 8), (1, 4))),
        "pattern": draw_pattern(jax.random.fold_in(key_of[4], 71), 0),
        "local_src": centred(key_of[2], (NX, NY, NB, S, 2 * TR), 0.5, 4.0, ((0, 8), (1, 4))),
        "owner": set_ends(jax.random.randint(key_of[3], (NB, S), 0, NX * NY), jax.random.fold_in(key_of[3], 1), 0, (NX * NY) - 1).astype(jnp.int32),
    }


def cell_matrix(blk, pat):
    dense = jnp.zeros((NBLK * NBLK, BS, BS), blk.dtype).at[pat].set(blk)
    return dense.reshape(NBLK, NBLK, BS, BS).transpose(0, 2, 1, 3).reshape(2 * TR, 2 * TR)


def reference(blocks, pattern, local_src, owner):
    cell_ids = jnp.arange(NX * NY, dtype=jnp.int32).reshape(NX, NY)

    def column(left_all, column_data):
        blk_col, pat_col, src_col, id_col = column_data

        def cell(bottom, cell_data):
            left, blk, pat, src, cell_id = cell_data
            joined = jnp.concatenate([left, bottom], axis=2).reshape(NB * S, 2 * TR)
            matrix = cell_matrix(blk, pat)
            total = jnp.dot(joined, matrix.T, preferred_element_type=jnp.float32).reshape(NB, S, 2 * TR)
            mask = (owner == cell_id).astype(jnp.float32)
            total = total + src.astype(jnp.float32) * mask[:, :, None]
            result = total.astype(jnp.bfloat16)
            return result[:, :, TR:], result

        zero = jnp.zeros((NB, S, TR), jnp.bfloat16)
        _, results = lax.scan(cell, zero, (left_all, blk_col, pat_col, src_col, id_col))
        return results[:, :, :, :TR], results

    start = jnp.zeros((NY, NB, S, TR), jnp.bfloat16)
    _, outputs = lax.scan(column, start, (blocks, pattern, local_src, cell_ids))
    return outputs
```

```python
import functools

import jax
import jax.numpy as jnp
from jax import lax
from jax.experimental import pallas as pl
from jax.experimental.pallas import tpu as pltpu
from jax.sharding import PartitionSpec as P

MESH = pl.DeviceIdType.MESH
GROUPS = 2
CHUNK = 256
PARTS = 4
UNROLL = 16
HEAD = 2
LEFT, BOTTOM = 0, 1


def kernel(
    dims,
    blocks_hbm,
    pattern_hbm,
    src_hbm,
    owner_hbm,
    out_ref,
    blk,
    pat_v,
    own_v,
    src_v,
    inv_v,
    inv_s,
    acc,
    inbuf,
    outbuf,
    relay,
    load_sem,
    send_sem,
    recv_sem,
    relay_send,
    relay_recv,
    onward_sem,
):
    nx, ny, nnz, order, rows, width = dims
    trace = width // 2
    nblk = width // order
    group = rows // GROUPS
    per_dir = trace // CHUNK
    sub = CHUNK // order
    me_x = lax.axis_index("gx")
    me_y = lax.axis_index("gy")
    has = (me_x > 0, me_y > 0)
    sends = (me_x < nx - 1, me_y < ny - 1)
    before = ((me_x - 1, me_y), (me_x, me_y - 1))
    after = ((me_x + 1, me_y), (me_x, me_y + 1))

    relayed = nx > 1 and ny > 1
    origin = jnp.logical_and(me_x == 0, me_y == 0)
    helper = jnp.logical_and(me_x == 1, me_y == 0)
    above_origin = jnp.logical_and(me_x == 0, me_y == 1)
    if relayed:
        before_y = (jnp.where(above_origin, 1, me_x), me_y - 1)
        before = (before[0], before_y)

    barrier = pltpu.get_barrier_semaphore()
    for d in range(2):

        @pl.when(has[d])
        def _():
            pl.semaphore_signal(barrier, inc=1, device_id=before[d], device_id_type=MESH)

    pat_copy = pltpu.make_async_copy(pattern_hbm, pat_v, load_sem.at[0])
    own_copy = pltpu.make_async_copy(owner_hbm, own_v, load_sem.at[1])
    src_copy = pltpu.make_async_copy(src_hbm, src_v, load_sem.at[2])
    pat_copy.start()
    own_copy.start()
    src_copy.start()
    step = nnz // PARTS
    blk_copies = [
        pltpu.make_async_copy(
            blocks_hbm.at[pl.ds(p * step, step)],
            blk.at[pl.ds(p * step, step)],
            load_sem.at[3 + p],
        )
        for p in range(PARTS)
    ]
    for copy in blk_copies:
        copy.start()
    blk[nnz] = jnp.zeros((order, order), blk.dtype)

    own_copy.wait()
    src_copy.wait()
    cell_id = me_x * ny + me_y
    nbatch, nsource = own_v.shape
    eye = lax.broadcasted_iota(jnp.int32, (nsource, nsource), 0) == lax.broadcasted_iota(
        jnp.int32, (nsource, nsource), 1
    )
    for b in range(nbatch):
        mine = (own_v[b : b + 1, :] == cell_id).astype(jnp.float32)
        mask = jnp.sum(jnp.where(eye, mine, 0.0), axis=1, keepdims=True)
        span = pl.ds(b * nsource, nsource)
        acc[span, :] = src_v[span, :].astype(jnp.float32) * mask

    wanted = sum(s.astype(jnp.int32) for s in sends)
    if relayed:
        wanted = wanted + helper.astype(jnp.int32) - origin.astype(jnp.int32)

    @pl.when(wanted > 0)
    def _():
        pl.semaphore_wait(barrier, wanted)

    def transfer(g, d, c):
        return pltpu.make_async_remote_copy(
            src_ref=outbuf.at[g, d, c],
            dst_ref=inbuf.at[g, d, c],
            send_sem=send_sem.at[g, d, c],
            recv_sem=recv_sem.at[g, d, c],
            device_id=after[d],
            device_id_type=MESH,
        )

    def weights(o, k):
        rows_of = []
        for b in range(sub):
            parts = []
            for a in range(sub):
                f = (o * sub + a) * nblk + k * sub + b
                parts.append(blk[inv_s[f // nnz, f % nnz]])
            rows_of.append(jnp.concatenate(parts, axis=1))
        return jnp.concatenate(rows_of, axis=0)

    def as_stored(o, k):
        rows_of = []
        for a in range(sub):
            f = (o * sub + a) * nblk + k * sub
            parts = [blk[inv_s[(f + b) // nnz, (f + b) % nnz]] for b in range(sub)]
            rows_of.append(jnp.concatenate(parts, axis=1))
        return jnp.concatenate(rows_of, axis=0)

    def product(g, d, c, outs):
        wide = [weights(o, d * per_dir + c) for o in outs]
        return jnp.dot(
            inbuf[g, d, c],
            jnp.concatenate(wide, axis=1),
            preferred_element_type=jnp.float32,
        )

    def stored_product(c, outs):
        tall = [as_stored(o, c) for o in outs]
        return lax.dot_general(
            jnp.concatenate([inbuf[g, LEFT, c] for g in range(GROUPS)], axis=0),
            jnp.concatenate(tall, axis=0),
            (((1,), (1,)), ((), ())),
            preferred_element_type=jnp.float32,
        )

    def handed(g, c):
        return pltpu.make_async_remote_copy(
            src_ref=outbuf.at[g, BOTTOM, c],
            dst_ref=relay.at[g, c],
            send_sem=relay_send.at[g, c],
            recv_sem=relay_recv.at[g, c],
            device_id=(me_x + 1, me_y),
            device_id_type=MESH,
        )

    def onward(g, c):
        return pltpu.make_async_remote_copy(
            src_ref=relay.at[g, c],
            dst_ref=inbuf.at[g, BOTTOM, c],
            send_sem=onward_sem.at[g, c],
            recv_sem=recv_sem.at[g, BOTTOM, c],
            device_id=(me_x - 1, me_y + 1),
            device_id_type=MESH,
        )

    def place(g, d, c):
        return (pl.ds(g * group, group), pl.ds((d * per_dir + c) * CHUNK, CHUNK))

    def store(g, d, c, value):
        result = value.astype(jnp.bfloat16)
        outbuf[g, d, c] = result
        out_ref[place(g, d, c)] = result

    def send(g, d, c):
        @pl.when(sends[d])
        def _():
            transfer(g, d, c).start()

    def emit(g, d, c, value):
        store(g, d, c, value)
        send(g, d, c)

    pairs = [((LEFT, c), (BOTTOM, c)) for c in range(per_dir)]

    def number(pair):
        return tuple(d * per_dir + c for d, c in pair)

    ordered = [(d, c) for c in range(per_dir) for d in (BOTTOM, LEFT)]
    any_input = jnp.logical_or(has[0], has[1])

    @pl.when(jnp.logical_not(any_input))
    def _():
        for g in range(GROUPS):
            for d, c in ordered:
                if relayed and d == BOTTOM:
                    store(g, d, c, acc[place(g, d, c)])
                    handed(g, c).start()
                else:
                    emit(g, d, c, acc[place(g, d, c)])
        pat_copy.wait()
        for copy in blk_copies:
            copy.wait()

    @pl.when(any_input)
    def _():
        pat_copy.wait()
        pat_t = jnp.transpose(jnp.broadcast_to(pat_v[...], (nnz, nnz)))
        lane = lax.broadcasted_iota(jnp.int32, (nnz, nnz), 1)
        which = lax.broadcasted_iota(jnp.int32, (nnz, nnz), 0)
        for h in range(nblk * nblk // nnz):
            hit = jnp.where(pat_t == lane + h * nnz, which, nnz)
            inv_v[h : h + 1, :] = jnp.min(hit, axis=0, keepdims=True)
        inv_copy = pltpu.make_async_copy(inv_v, inv_s, load_sem.at[3 + PARTS])
        inv_copy.start()
        if relayed:

            @pl.when(helper)
            def _():
                for g in range(GROUPS):
                    for c in range(per_dir):
                        handed(g, c).wait_recv()
                        onward(g, c).start()

        inv_copy.wait()

        for p, copy in enumerate(blk_copies):
            copy.wait()

            def turn(i, carry):
                for u in range(UNROLL):
                    at = p * step + i * UNROLL + u
                    blk[at] = jnp.transpose(blk[at])
                return carry

            @pl.when(jnp.logical_not(helper))
            def _():
                lax.fori_loop(0, step // UNROLL, turn, 0)

        def gather(g, d, c):
            transfer(g, d, c).wait_recv()
            for pair in pairs:
                both = product(g, d, c, number(pair))
                for n, (od, oc) in enumerate(pair):
                    at = place(g, od, oc)
                    acc[at] = acc[at] + both[:, n * CHUNK : (n + 1) * CHUNK]

        def apply(g, dirs):
            for d in dirs[:-1]:
                for c in range(per_dir):
                    gather(g, d, c)
            d = dirs[-1]
            for c in range(HEAD):
                gather(g, d, c)
            for c in range(HEAD, per_dir):
                transfer(g, d, c).wait_recv()
            for pair in pairs:
                both = sum(product(g, d, c, number(pair)) for c in range(HEAD, per_dir))
                for n, (od, oc) in enumerate(pair):
                    value = acc[place(g, od, oc)] + both[:, n * CHUNK : (n + 1) * CHUNK]
                    emit(g, od, oc, value)

        for dirs in ((BOTTOM, LEFT), (LEFT,), (BOTTOM,)):
            here = [has[d] if d in dirs else jnp.logical_not(has[d]) for d in range(2)]
            here = jnp.logical_and(jnp.logical_and(here[0], here[1]), jnp.logical_not(helper))

            @pl.when(here)
            def _():
                for g in range(GROUPS):
                    apply(g, dirs)

        @pl.when(helper)
        def _():
            for g in range(GROUPS):
                for c in range(per_dir):
                    transfer(g, LEFT, c).wait_recv()
            for pair in [((d, c), (d, c + 1)) for d in range(2) for c in range(0, per_dir, 2)]:
                both = sum(stored_product(c, number(pair)) for c in range(per_dir))
                for g in range(GROUPS):
                    for n, (od, oc) in enumerate(pair):
                        part = both[g * group : (g + 1) * group, n * CHUNK : (n + 1) * CHUNK]
                        emit(g, od, oc, acc[place(g, od, oc)] + part)

    for g in range(GROUPS):
        for d in (LEFT, BOTTOM):
            for c in range(per_dir):
                if relayed and d == BOTTOM:

                    @pl.when(jnp.logical_and(sends[d], jnp.logical_not(origin)))
                    def _():
                        transfer(g, d, c).wait_send()

                    @pl.when(origin)
                    def _():
                        handed(g, c).wait_send()

                    @pl.when(helper)
                    def _():
                        onward(g, c).wait_send()

                else:

                    @pl.when(sends[d])
                    def _():
                        transfer(g, d, c).wait_send()


def body(nx, ny, blocks, pattern, local_src, owner):
    nnz, order = blocks.shape[2], blocks.shape[3]
    nbatch, nsource, width = local_src.shape[2:]
    rows = nbatch * nsource
    nblk = width // order
    per_dir = width // 2 // CHUNK
    group = rows // GROUPS
    dims = (nx, ny, nnz, order, rows, width)
    any_spec = pl.BlockSpec(memory_space=pl.ANY)
    result = pl.pallas_call(
        functools.partial(kernel, dims),
        name="sweep",
        out_shape=pltpu.VMEM((rows, width), jnp.bfloat16),
        in_specs=[any_spec] * 4,
        out_specs=pl.BlockSpec(memory_space=pltpu.VMEM),
        scratch_shapes=[
            pltpu.VMEM((nnz + 1, order, order), jnp.bfloat16),
            pltpu.VMEM((1, nnz), jnp.int32),
            pltpu.VMEM((nbatch, nsource), jnp.int32),
            pltpu.VMEM((rows, width), jnp.bfloat16),
            pltpu.VMEM((nblk * nblk // nnz, nnz), jnp.int32),
            pltpu.SMEM((nblk * nblk // nnz, nnz), jnp.int32),
            pltpu.VMEM((rows, width), jnp.float32),
            pltpu.VMEM((GROUPS, 2, per_dir, group, CHUNK), jnp.bfloat16),
            pltpu.VMEM((GROUPS, 2, per_dir, group, CHUNK), jnp.bfloat16),
            pltpu.VMEM((GROUPS, per_dir, group, CHUNK), jnp.bfloat16),
            pltpu.SemaphoreType.DMA((4 + PARTS,)),
            pltpu.SemaphoreType.DMA((GROUPS, 2, per_dir)),
            pltpu.SemaphoreType.DMA((GROUPS, 2, per_dir)),
            pltpu.SemaphoreType.DMA((GROUPS, per_dir)),
            pltpu.SemaphoreType.DMA((GROUPS, per_dir)),
            pltpu.SemaphoreType.DMA((GROUPS, per_dir)),
        ],
        compiler_params=pltpu.CompilerParams(collective_id=0, has_side_effects=True),
    )(
        blocks.reshape(nnz, order, order),
        pattern.reshape(1, nnz),
        local_src.reshape(rows, width),
        owner,
    )
    return result.reshape(1, 1, nbatch, nsource, width)


def solution(mesh):
    return jax.shard_map(
        functools.partial(body, mesh.shape["gx"], mesh.shape["gy"]),
        mesh=mesh,
        in_specs=(
            P("gx", "gy", None, None, None),
            P("gx", "gy", None),
            P("gx", "gy", None, None, None),
            P(),
        ),
        out_specs=P("gx", "gy", None, None, None),
        check_vma=False,
    )
```

```python
import functools

import jax
import jax.numpy as jnp
from jax import lax
from jax.experimental import pallas as pl
from jax.experimental.pallas import tpu as pltpu
from jax.sharding import PartitionSpec as P

MESH = pl.DeviceIdType.MESH
GROUPS = 2
CHUNK = 256
PARTS = 4
UNROLL = 16
HEAD = 2
LEFT, BOTTOM = 0, 1


def kernel(
    dims,
    blocks_hbm,
    pattern_hbm,
    src_hbm,
    owner_hbm,
    out_ref,
    blk,
    pat_v,
    own_v,
    src_v,
    inv_v,
    inv_s,
    acc,
    inbuf,
    outbuf,
    relay,
    load_sem,
    send_sem,
    recv_sem,
    relay_send,
    relay_recv,
    onward_sem,
):
    nx, ny, nnz, order, rows, width = dims
    trace = width // 2
    nblk = width // order
    group = rows // GROUPS
    per_dir = trace // CHUNK
    sub = CHUNK // order
    me_x = lax.axis_index("gx")
    me_y = lax.axis_index("gy")
    has = (me_x > 0, me_y > 0)
    sends = (me_x < nx - 1, me_y < ny - 1)
    before = ((me_x - 1, me_y), (me_x, me_y - 1))
    after = ((me_x + 1, me_y), (me_x, me_y + 1))

    relayed = nx > 1 and ny > 1
    origin = jnp.logical_and(me_x == 0, me_y == 0)
    helper = jnp.logical_and(me_x == 1, me_y == 0)
    above_origin = jnp.logical_and(me_x == 0, me_y == 1)
    if relayed:
        before_y = (jnp.where(above_origin, 1, me_x), me_y - 1)
        before = (before[0], before_y)

    barrier = pltpu.get_barrier_semaphore()
    for d in range(2):

        @pl.when(has[d])
        def _():
            pl.semaphore_signal(barrier, inc=1, device_id=before[d], device_id_type=MESH)

    pat_copy = pltpu.make_async_copy(pattern_hbm, pat_v, load_sem.at[0])
    own_copy = pltpu.make_async_copy(owner_hbm, own_v, load_sem.at[1])
    src_copy = pltpu.make_async_copy(src_hbm, src_v, load_sem.at[2])
    pat_copy.start()
    own_copy.start()
    src_copy.start()
    step = nnz // PARTS
    blk_copies = [
        pltpu.make_async_copy(
            blocks_hbm.at[pl.ds(p * step, step)],
            blk.at[pl.ds(p * step, step)],
            load_sem.at[3 + p],
        )
        for p in range(PARTS)
    ]
    for copy in blk_copies:
        copy.start()
    blk[nnz] = jnp.zeros((order, order), blk.dtype)

    own_copy.wait()
    src_copy.wait()
    cell_id = me_x * ny + me_y
    nbatch, nsource = own_v.shape
    eye = lax.broadcasted_iota(jnp.int32, (nsource, nsource), 0) == lax.broadcasted_iota(
        jnp.int32, (nsource, nsource), 1
    )
    for b in range(nbatch):
        mine = (own_v[b : b + 1, :] == cell_id).astype(jnp.float32)
        mask = jnp.sum(jnp.where(eye, mine, 0.0), axis=1, keepdims=True)
        span = pl.ds(b * nsource, nsource)
        acc[span, :] = src_v[span, :].astype(jnp.float32) * mask

    wanted = sum(s.astype(jnp.int32) for s in sends)
    if relayed:
        wanted = wanted + helper.astype(jnp.int32) - origin.astype(jnp.int32)

    @pl.when(wanted > 0)
    def _():
        pl.semaphore_wait(barrier, wanted)

    def transfer(g, d, c):
        return pltpu.make_async_remote_copy(
            src_ref=outbuf.at[g, d, c],
            dst_ref=inbuf.at[g, d, c],
            send_sem=send_sem.at[g, d, c],
            recv_sem=recv_sem.at[g, d, c],
            device_id=after[d],
            device_id_type=MESH,
        )

    def weights(o, k):
        rows_of = []
        for b in range(sub):
            parts = []
            for a in range(sub):
                f = (o * sub + a) * nblk + k * sub + b
                parts.append(blk[inv_s[f // nnz, f % nnz]])
            rows_of.append(jnp.concatenate(parts, axis=1))
        return jnp.concatenate(rows_of, axis=0)

    def as_stored(o, k):
        rows_of = []
        for a in range(sub):
            f = (o * sub + a) * nblk + k * sub
            parts = [blk[inv_s[(f + b) // nnz, (f + b) % nnz]] for b in range(sub)]
            rows_of.append(jnp.concatenate(parts, axis=1))
        return jnp.concatenate(rows_of, axis=0)

    def product(g, d, c, outs):
        wide = [weights(o, d * per_dir + c) for o in outs]
        return jnp.dot(
            inbuf[g, d, c],
            jnp.concatenate(wide, axis=1),
            preferred_element_type=jnp.float32,
        )

    def whole(d, c):
        return jnp.concatenate([inbuf[g, d, c] for g in range(GROUPS)], axis=0)

    def whole_product(d, c, outs):
        wide = [weights(o, d * per_dir + c) for o in outs]
        return jnp.dot(
            whole(d, c), jnp.concatenate(wide, axis=1), preferred_element_type=jnp.float32
        )

    def stored_product(c, outs):
        tall = [as_stored(o, c) for o in outs]
        return lax.dot_general(
            whole(LEFT, c),
            jnp.concatenate(tall, axis=0),
            (((1,), (1,)), ((), ())),
            preferred_element_type=jnp.float32,
        )

    def handed(g, c):
        return pltpu.make_async_remote_copy(
            src_ref=outbuf.at[g, BOTTOM, c],
            dst_ref=relay.at[g, c],
            send_sem=relay_send.at[g, c],
            recv_sem=relay_recv.at[g, c],
            device_id=(me_x + 1, me_y),
            device_id_type=MESH,
        )

    def onward(g, c):
        return pltpu.make_async_remote_copy(
            src_ref=relay.at[g, c],
            dst_ref=inbuf.at[g, BOTTOM, c],
            send_sem=onward_sem.at[g, c],
            recv_sem=recv_sem.at[g, BOTTOM, c],
            device_id=(me_x - 1, me_y + 1),
            device_id_type=MESH,
        )

    def place(g, d, c):
        return (pl.ds(g * group, group), pl.ds((d * per_dir + c) * CHUNK, CHUNK))

    def store(g, d, c, value):
        result = value.astype(jnp.bfloat16)
        outbuf[g, d, c] = result
        out_ref[place(g, d, c)] = result

    def send(g, d, c):
        @pl.when(sends[d])
        def _():
            transfer(g, d, c).start()

    def emit(g, d, c, value):
        store(g, d, c, value)
        send(g, d, c)

    pairs = [((LEFT, c), (BOTTOM, c)) for c in range(per_dir)]
    sideways, upwards = (
        [((d, c), (d, c + 1)) for c in range(0, per_dir, 2)] for d in (LEFT, BOTTOM)
    )

    def number(pair):
        return tuple(d * per_dir + c for d, c in pair)

    ordered = [(d, c) for c in range(per_dir) for d in (BOTTOM, LEFT)]
    any_input = jnp.logical_or(has[0], has[1])

    @pl.when(jnp.logical_not(any_input))
    def _():
        for g in range(GROUPS):
            for d, c in ordered:
                if relayed and d == BOTTOM:
                    store(g, d, c, acc[place(g, d, c)])
                    handed(g, c).start()
                else:
                    emit(g, d, c, acc[place(g, d, c)])
        pat_copy.wait()
        for copy in blk_copies:
            copy.wait()

    @pl.when(any_input)
    def _():
        pat_copy.wait()
        pat_t = jnp.transpose(jnp.broadcast_to(pat_v[...], (nnz, nnz)))
        lane = lax.broadcasted_iota(jnp.int32, (nnz, nnz), 1)
        which = lax.broadcasted_iota(jnp.int32, (nnz, nnz), 0)
        for h in range(nblk * nblk // nnz):
            hit = jnp.where(pat_t == lane + h * nnz, which, nnz)
            inv_v[h : h + 1, :] = jnp.min(hit, axis=0, keepdims=True)
        inv_copy = pltpu.make_async_copy(inv_v, inv_s, load_sem.at[3 + PARTS])
        inv_copy.start()
        if relayed:

            @pl.when(helper)
            def _():
                for g in range(GROUPS):
                    for c in range(per_dir):
                        handed(g, c).wait_recv()
                        onward(g, c).start()

        inv_copy.wait()

        for p, copy in enumerate(blk_copies):
            copy.wait()

            def turn(i, carry):
                for u in range(UNROLL):
                    at = p * step + i * UNROLL + u
                    blk[at] = jnp.transpose(blk[at])
                return carry

            @pl.when(jnp.logical_not(helper))
            def _():
                lax.fori_loop(0, step // UNROLL, turn, 0)

        def gather(g, d, c, outs):
            transfer(g, d, c).wait_recv()
            for pair in outs:
                both = product(g, d, c, number(pair))
                for n, (od, oc) in enumerate(pair):
                    at = place(g, od, oc)
                    acc[at] = acc[at] + both[:, n * CHUNK : (n + 1) * CHUNK]

        def finish(g, last, outs):
            for d, c in last:
                transfer(g, d, c).wait_recv()
            for pair in outs:
                both = sum(product(g, d, c, number(pair)) for d, c in last)
                for n, (od, oc) in enumerate(pair):
                    value = acc[place(g, od, oc)] + both[:, n * CHUNK : (n + 1) * CHUNK]
                    emit(g, od, oc, value)

        def split(dirs):
            early = [(d, c) for d in dirs[:-1] for c in range(per_dir)]
            early += [(dirs[-1], c) for c in range(HEAD)]
            return early, [(dirs[-1], c) for c in range(HEAD, per_dir)]

        def anywhere(dirs):
            early, last = split(dirs)
            for g in range(GROUPS):
                for d, c in early:
                    gather(g, d, c, pairs)
                finish(g, last, pairs)

        def top_row(dirs):
            early, last = split(dirs)
            for g in range(GROUPS):
                for d, c in early:
                    gather(g, d, c, sideways)
                finish(g, last, sideways)
            for pair in upwards:
                both = sum(whole_product(d, c, number(pair)) for d, c in early + last)
                for n, (od, oc) in enumerate(pair):
                    at = (slice(None), pl.ds((od * per_dir + oc) * CHUNK, CHUNK))
                    value = acc[at] + both[:, n * CHUNK : (n + 1) * CHUNK]
                    out_ref[at] = value.astype(jnp.bfloat16)

        def across(pair):
            return [
                (slice(None), pl.ds((od * per_dir + oc) * CHUNK, CHUNK)) for od, oc in pair
            ]

        def last_cell(dirs):
            early, last = split(dirs)
            for g in range(GROUPS):
                for d, c in early:
                    if d == dirs[0]:
                        gather(g, d, c, pairs)
            for d, c in early:
                if d != dirs[0]:
                    for g in range(GROUPS):
                        transfer(g, d, c).wait_recv()
                    for pair in pairs:
                        both = whole_product(d, c, number(pair))
                        for n, at in enumerate(across(pair)):
                            acc[at] = acc[at] + both[:, n * CHUNK : (n + 1) * CHUNK]
            for d, c in last:
                for g in range(GROUPS):
                    transfer(g, d, c).wait_recv()
            for pair in pairs:
                both = sum(whole_product(d, c, number(pair)) for d, c in last)
                for n, at in enumerate(across(pair)):
                    value = acc[at] + both[:, n * CHUNK : (n + 1) * CHUNK]
                    out_ref[at] = value.astype(jnp.bfloat16)

        top = jnp.logical_and(has[BOTTOM], jnp.logical_not(sends[BOTTOM]))
        end = jnp.logical_and(jnp.logical_and(top, has[LEFT]), jnp.logical_not(sends[LEFT]))
        below = jnp.logical_not(top)
        plans = (
            (below, (BOTTOM, LEFT), anywhere),
            (below, (LEFT,), anywhere),
            (below, (BOTTOM,), anywhere),
            (jnp.logical_and(top, jnp.logical_not(end)), (BOTTOM, LEFT), top_row),
            (top, (BOTTOM,), top_row),
            (end, (BOTTOM, LEFT), last_cell),
        )
        for where, dirs, plan in plans:
            here = [has[d] if d in dirs else jnp.logical_not(has[d]) for d in range(2)]
            here = jnp.logical_and(jnp.logical_and(here[0], here[1]), jnp.logical_not(helper))

            @pl.when(jnp.logical_and(here, where))
            def _():
                plan(dirs)

        @pl.when(helper)
        def _():
            for g in range(GROUPS):
                for c in range(per_dir):
                    transfer(g, LEFT, c).wait_recv()
            for pair in sideways + upwards:
                both = sum(stored_product(c, number(pair)) for c in range(per_dir))
                for g in range(GROUPS):
                    for n, (od, oc) in enumerate(pair):
                        part = both[g * group : (g + 1) * group, n * CHUNK : (n + 1) * CHUNK]
                        emit(g, od, oc, acc[place(g, od, oc)] + part)

    for g in range(GROUPS):
        for d in (LEFT, BOTTOM):
            for c in range(per_dir):
                if relayed and d == BOTTOM:

                    @pl.when(jnp.logical_and(sends[d], jnp.logical_not(origin)))
                    def _():
                        transfer(g, d, c).wait_send()

                    @pl.when(origin)
                    def _():
                        handed(g, c).wait_send()

                    @pl.when(helper)
                    def _():
                        onward(g, c).wait_send()

                else:

                    @pl.when(sends[d])
                    def _():
                        transfer(g, d, c).wait_send()


def body(nx, ny, blocks, pattern, local_src, owner):
    nnz, order = blocks.shape[2], blocks.shape[3]
    nbatch, nsource, width = local_src.shape[2:]
    rows = nbatch * nsource
    nblk = width // order
    per_dir = width // 2 // CHUNK
    group = rows // GROUPS
    dims = (nx, ny, nnz, order, rows, width)
    any_spec = pl.BlockSpec(memory_space=pl.ANY)
    result = pl.pallas_call(
        functools.partial(kernel, dims),
        name="sweep",
        out_shape=pltpu.VMEM((rows, width), jnp.bfloat16),
        in_specs=[any_spec] * 4,
        out_specs=pl.BlockSpec(memory_space=pltpu.VMEM),
        scratch_shapes=[
            pltpu.VMEM((nnz + 1, order, order), jnp.bfloat16),
            pltpu.VMEM((1, nnz), jnp.int32),
            pltpu.VMEM((nbatch, nsource), jnp.int32),
            pltpu.VMEM((rows, width), jnp.bfloat16),
            pltpu.VMEM((nblk * nblk // nnz, nnz), jnp.int32),
            pltpu.SMEM((nblk * nblk // nnz, nnz), jnp.int32),
            pltpu.VMEM((rows, width), jnp.float32),
            pltpu.VMEM((GROUPS, 2, per_dir, group, CHUNK), jnp.bfloat16),
            pltpu.VMEM((GROUPS, 2, per_dir, group, CHUNK), jnp.bfloat16),
            pltpu.VMEM((GROUPS, per_dir, group, CHUNK), jnp.bfloat16),
            pltpu.SemaphoreType.DMA((4 + PARTS,)),
            pltpu.SemaphoreType.DMA((GROUPS, 2, per_dir)),
            pltpu.SemaphoreType.DMA((GROUPS, 2, per_dir)),
            pltpu.SemaphoreType.DMA((GROUPS, per_dir)),
            pltpu.SemaphoreType.DMA((GROUPS, per_dir)),
            pltpu.SemaphoreType.DMA((GROUPS, per_dir)),
        ],
        compiler_params=pltpu.CompilerParams(collective_id=0, has_side_effects=True),
    )(
        blocks.reshape(nnz, order, order),
        pattern.reshape(1, nnz),
        local_src.reshape(rows, width),
        owner,
    )
    return result.reshape(1, 1, nbatch, nsource, width)


def solution(mesh):
    return jax.shard_map(
        functools.partial(body, mesh.shape["gx"], mesh.shape["gy"]),
        mesh=mesh,
        in_specs=(
            P("gx", "gy", None, None, None),
            P("gx", "gy", None),
            P("gx", "gy", None, None, None),
            P(),
        ),
        out_specs=P("gx", "gy", None, None, None),
        check_vma=False,
    )
```

```python
import functools

import jax
import jax.numpy as jnp
from jax import lax
from jax.experimental import pallas as pl
from jax.experimental.pallas import tpu as pltpu
from jax.sharding import PartitionSpec as P

MESH = pl.DeviceIdType.MESH
GROUPS = 2
CHUNK = 256
PARTS = 4
UNROLL = 16
HEAD = 2
LEFT, BOTTOM = 0, 1


def kernel(
    dims,
    blocks_hbm,
    pattern_hbm,
    src_hbm,
    owner_hbm,
    out_ref,
    blk,
    pat_v,
    own_v,
    src_v,
    inv_v,
    inv_s,
    acc,
    inbuf,
    outbuf,
    relay,
    load_sem,
    send_sem,
    recv_sem,
    relay_send,
    relay_recv,
    onward_sem,
):
    nx, ny, nnz, order, rows, width = dims
    trace = width // 2
    nblk = width // order
    group = rows // GROUPS
    per_dir = trace // CHUNK
    sub = CHUNK // order
    me_x = lax.axis_index("gx")
    me_y = lax.axis_index("gy")
    has = (me_x > 0, me_y > 0)
    sends = (me_x < nx - 1, me_y < ny - 1)
    before = ((me_x - 1, me_y), (me_x, me_y - 1))
    after = ((me_x + 1, me_y), (me_x, me_y + 1))

    relayed = nx > 1 and ny > 1
    origin = jnp.logical_and(me_x == 0, me_y == 0)
    helper = jnp.logical_and(me_x == 1, me_y == 0)
    above_origin = jnp.logical_and(me_x == 0, me_y == 1)
    if relayed:
        before_y = (jnp.where(above_origin, 1, me_x), me_y - 1)
        before = (before[0], before_y)

    barrier = pltpu.get_barrier_semaphore()
    for d in range(2):

        @pl.when(has[d])
        def _():
            pl.semaphore_signal(barrier, inc=1, device_id=before[d], device_id_type=MESH)

    pat_copy = pltpu.make_async_copy(pattern_hbm, pat_v, load_sem.at[0])
    own_copy = pltpu.make_async_copy(owner_hbm, own_v, load_sem.at[1])
    src_copy = pltpu.make_async_copy(src_hbm, src_v, load_sem.at[2])
    pat_copy.start()
    own_copy.start()
    src_copy.start()
    step = nnz // PARTS
    blk_copies = [
        pltpu.make_async_copy(
            blocks_hbm.at[pl.ds(p * step, step)],
            blk.at[pl.ds(p * step, step)],
            load_sem.at[3 + p],
        )
        for p in range(PARTS)
    ]
    for copy in blk_copies:
        copy.start()
    blk[nnz] = jnp.zeros((order, order), blk.dtype)

    any_input = jnp.logical_or(has[0], has[1])
    inv_copy = pltpu.make_async_copy(inv_v, inv_s, load_sem.at[3 + PARTS])

    @pl.when(any_input)
    def _():
        pat_copy.wait()
        pat_t = jnp.transpose(jnp.broadcast_to(pat_v[...], (nnz, nnz)))
        lane = lax.broadcasted_iota(jnp.int32, (nnz, nnz), 1)
        which = lax.broadcasted_iota(jnp.int32, (nnz, nnz), 0)
        for h in range(nblk * nblk // nnz):
            hit = jnp.where(pat_t == lane + h * nnz, which, nnz)
            inv_v[h : h + 1, :] = jnp.min(hit, axis=0, keepdims=True)
        inv_copy.start()

    own_copy.wait()
    src_copy.wait()
    cell_id = me_x * ny + me_y
    nbatch, nsource = own_v.shape
    eye = lax.broadcasted_iota(jnp.int32, (nsource, nsource), 0) == lax.broadcasted_iota(
        jnp.int32, (nsource, nsource), 1
    )
    for b in range(nbatch):
        mine = (own_v[b : b + 1, :] == cell_id).astype(jnp.float32)
        mask = jnp.sum(jnp.where(eye, mine, 0.0), axis=1, keepdims=True)
        span = pl.ds(b * nsource, nsource)
        acc[span, :] = src_v[span, :].astype(jnp.float32) * mask

    @pl.when(jnp.logical_and(any_input, jnp.logical_not(helper)))
    def _():
        for p, copy in enumerate(blk_copies):
            copy.wait()

            def turn(i, carry):
                for u in range(UNROLL):
                    at = p * step + i * UNROLL + u
                    blk[at] = jnp.transpose(blk[at])
                return carry

            lax.fori_loop(0, step // UNROLL, turn, 0)

    wanted = sum(s.astype(jnp.int32) for s in sends)
    if relayed:
        wanted = wanted + helper.astype(jnp.int32) - origin.astype(jnp.int32)

    @pl.when(wanted > 0)
    def _():
        pl.semaphore_wait(barrier, wanted)

    def transfer(g, d, c):
        return pltpu.make_async_remote_copy(
            src_ref=outbuf.at[g, d, c],
            dst_ref=inbuf.at[g, d, c],
            send_sem=send_sem.at[g, d, c],
            recv_sem=recv_sem.at[g, d, c],
            device_id=after[d],
            device_id_type=MESH,
        )

    def weights(o, k):
        rows_of = []
        for b in range(sub):
            parts = []
            for a in range(sub):
                f = (o * sub + a) * nblk + k * sub + b
                parts.append(blk[inv_s[f // nnz, f % nnz]])
            rows_of.append(jnp.concatenate(parts, axis=1))
        return jnp.concatenate(rows_of, axis=0)

    def as_stored(o, k):
        rows_of = []
        for a in range(sub):
            f = (o * sub + a) * nblk + k * sub
            parts = [blk[inv_s[(f + b) // nnz, (f + b) % nnz]] for b in range(sub)]
            rows_of.append(jnp.concatenate(parts, axis=1))
        return jnp.concatenate(rows_of, axis=0)

    def product(g, d, c, outs):
        wide = [weights(o, d * per_dir + c) for o in outs]
        return jnp.dot(
            inbuf[g, d, c],
            jnp.concatenate(wide, axis=1),
            preferred_element_type=jnp.float32,
        )

    def whole(d, c):
        return jnp.concatenate([inbuf[g, d, c] for g in range(GROUPS)], axis=0)

    def whole_product(d, c, outs):
        wide = [weights(o, d * per_dir + c) for o in outs]
        return jnp.dot(
            whole(d, c), jnp.concatenate(wide, axis=1), preferred_element_type=jnp.float32
        )

    def stored_product(c, outs):
        tall = [as_stored(o, c) for o in outs]
        return lax.dot_general(
            whole(LEFT, c),
            jnp.concatenate(tall, axis=0),
            (((1,), (1,)), ((), ())),
            preferred_element_type=jnp.float32,
        )

    def handed(g, c):
        return pltpu.make_async_remote_copy(
            src_ref=outbuf.at[g, BOTTOM, c],
            dst_ref=relay.at[g, c],
            send_sem=relay_send.at[g, c],
            recv_sem=relay_recv.at[g, c],
            device_id=(me_x + 1, me_y),
            device_id_type=MESH,
        )

    def onward(g, c):
        return pltpu.make_async_remote_copy(
            src_ref=relay.at[g, c],
            dst_ref=inbuf.at[g, BOTTOM, c],
            send_sem=onward_sem.at[g, c],
            recv_sem=recv_sem.at[g, BOTTOM, c],
            device_id=(me_x - 1, me_y + 1),
            device_id_type=MESH,
        )

    def place(g, d, c):
        return (pl.ds(g * group, group), pl.ds((d * per_dir + c) * CHUNK, CHUNK))

    def store(g, d, c, value):
        result = value.astype(jnp.bfloat16)
        outbuf[g, d, c] = result
        out_ref[place(g, d, c)] = result

    def send(g, d, c):
        @pl.when(sends[d])
        def _():
            transfer(g, d, c).start()

    def emit(g, d, c, value):
        store(g, d, c, value)
        send(g, d, c)

    pairs = [((LEFT, c), (BOTTOM, c)) for c in range(per_dir)]
    sideways, upwards = (
        [((d, c), (d, c + 1)) for c in range(0, per_dir, 2)] for d in (LEFT, BOTTOM)
    )

    def number(pair):
        return tuple(d * per_dir + c for d, c in pair)

    ordered = [(d, c) for c in range(per_dir) for d in (BOTTOM, LEFT)]
    @pl.when(jnp.logical_not(any_input))
    def _():
        for g in range(GROUPS):
            for d, c in ordered:
                if relayed and d == BOTTOM:
                    store(g, d, c, acc[place(g, d, c)])
                    handed(g, c).start()
                else:
                    emit(g, d, c, acc[place(g, d, c)])
        pat_copy.wait()
        for copy in blk_copies:
            copy.wait()

    @pl.when(any_input)
    def _():
        if relayed:

            @pl.when(helper)
            def _():
                for g in range(GROUPS):
                    for c in range(per_dir):
                        handed(g, c).wait_recv()
                        onward(g, c).start()

        @pl.when(helper)
        def _():
            for copy in blk_copies:
                copy.wait()

        inv_copy.wait()


        def gather(g, d, c, outs):
            transfer(g, d, c).wait_recv()
            for pair in outs:
                both = product(g, d, c, number(pair))
                for n, (od, oc) in enumerate(pair):
                    at = place(g, od, oc)
                    acc[at] = acc[at] + both[:, n * CHUNK : (n + 1) * CHUNK]

        def finish(g, last, outs):
            for d, c in last:
                transfer(g, d, c).wait_recv()
            for pair in outs:
                both = sum(product(g, d, c, number(pair)) for d, c in last)
                for n, (od, oc) in enumerate(pair):
                    value = acc[place(g, od, oc)] + both[:, n * CHUNK : (n + 1) * CHUNK]
                    emit(g, od, oc, value)

        def split(dirs):
            early = [(d, c) for d in dirs[:-1] for c in range(per_dir)]
            early += [(dirs[-1], c) for c in range(HEAD)]
            return early, [(dirs[-1], c) for c in range(HEAD, per_dir)]

        def anywhere(dirs):
            early, last = split(dirs)
            for g in range(GROUPS):
                for d, c in early:
                    gather(g, d, c, pairs)
                finish(g, last, pairs)

        def top_row(dirs):
            early, last = split(dirs)
            early, last = early + last[:-1], last[-1:]
            for g in range(GROUPS):
                for d, c in early:
                    gather(g, d, c, sideways)
                finish(g, last, sideways)
            for pair in upwards:
                both = sum(whole_product(d, c, number(pair)) for d, c in early + last)
                for n, (od, oc) in enumerate(pair):
                    at = (slice(None), pl.ds((od * per_dir + oc) * CHUNK, CHUNK))
                    value = acc[at] + both[:, n * CHUNK : (n + 1) * CHUNK]
                    out_ref[at] = value.astype(jnp.bfloat16)

        def across(pair):
            return [
                (slice(None), pl.ds((od * per_dir + oc) * CHUNK, CHUNK)) for od, oc in pair
            ]

        def last_cell(dirs):
            early, last = split(dirs)
            for g in range(GROUPS):
                for d, c in early:
                    if d == dirs[0]:
                        gather(g, d, c, pairs)
            for d, c in early:
                if d != dirs[0]:
                    for g in range(GROUPS):
                        transfer(g, d, c).wait_recv()
                    for pair in pairs:
                        both = whole_product(d, c, number(pair))
                        for n, at in enumerate(across(pair)):
                            acc[at] = acc[at] + both[:, n * CHUNK : (n + 1) * CHUNK]
            for d, c in last:
                for g in range(GROUPS):
                    transfer(g, d, c).wait_recv()
            for pair in pairs:
                both = sum(whole_product(d, c, number(pair)) for d, c in last)
                for n, at in enumerate(across(pair)):
                    value = acc[at] + both[:, n * CHUNK : (n + 1) * CHUNK]
                    out_ref[at] = value.astype(jnp.bfloat16)

        top = jnp.logical_and(has[BOTTOM], jnp.logical_not(sends[BOTTOM]))
        end = jnp.logical_and(jnp.logical_and(top, has[LEFT]), jnp.logical_not(sends[LEFT]))
        below = jnp.logical_not(top)
        plans = (
            (below, (BOTTOM, LEFT), anywhere),
            (below, (LEFT,), anywhere),
            (below, (BOTTOM,), anywhere),
            (jnp.logical_and(top, jnp.logical_not(end)), (BOTTOM, LEFT), top_row),
            (top, (BOTTOM,), top_row),
            (end, (BOTTOM, LEFT), last_cell),
        )
        for where, dirs, plan in plans:
            here = [has[d] if d in dirs else jnp.logical_not(has[d]) for d in range(2)]
            here = jnp.logical_and(jnp.logical_and(here[0], here[1]), jnp.logical_not(helper))

            @pl.when(jnp.logical_and(here, where))
            def _():
                plan(dirs)

        @pl.when(helper)
        def _():
            for g in range(GROUPS):
                for c in range(per_dir):
                    transfer(g, LEFT, c).wait_recv()
            for pair in sideways + upwards:
                both = sum(stored_product(c, number(pair)) for c in range(per_dir))
                for g in range(GROUPS):
                    for n, (od, oc) in enumerate(pair):
                        part = both[g * group : (g + 1) * group, n * CHUNK : (n + 1) * CHUNK]
                        emit(g, od, oc, acc[place(g, od, oc)] + part)

    for g in range(GROUPS):
        for d in (LEFT, BOTTOM):
            for c in range(per_dir):
                if relayed and d == BOTTOM:

                    @pl.when(jnp.logical_and(sends[d], jnp.logical_not(origin)))
                    def _():
                        transfer(g, d, c).wait_send()

                    @pl.when(origin)
                    def _():
                        handed(g, c).wait_send()

                    @pl.when(helper)
                    def _():
                        onward(g, c).wait_send()

                else:

                    @pl.when(sends[d])
                    def _():
                        transfer(g, d, c).wait_send()


def body(nx, ny, blocks, pattern, local_src, owner):
    nnz, order = blocks.shape[2], blocks.shape[3]
    nbatch, nsource, width = local_src.shape[2:]
    rows = nbatch * nsource
    nblk = width // order
    per_dir = width // 2 // CHUNK
    group = rows // GROUPS
    dims = (nx, ny, nnz, order, rows, width)
    any_spec = pl.BlockSpec(memory_space=pl.ANY)
    result = pl.pallas_call(
        functools.partial(kernel, dims),
        name="sweep",
        out_shape=pltpu.VMEM((rows, width), jnp.bfloat16),
        in_specs=[any_spec] * 4,
        out_specs=pl.BlockSpec(memory_space=pltpu.VMEM),
        scratch_shapes=[
            pltpu.VMEM((nnz + 1, order, order), jnp.bfloat16),
            pltpu.VMEM((1, nnz), jnp.int32),
            pltpu.VMEM((nbatch, nsource), jnp.int32),
            pltpu.VMEM((rows, width), jnp.bfloat16),
            pltpu.VMEM((nblk * nblk // nnz, nnz), jnp.int32),
            pltpu.SMEM((nblk * nblk // nnz, nnz), jnp.int32),
            pltpu.VMEM((rows, width), jnp.float32),
            pltpu.VMEM((GROUPS, 2, per_dir, group, CHUNK), jnp.bfloat16),
            pltpu.VMEM((GROUPS, 2, per_dir, group, CHUNK), jnp.bfloat16),
            pltpu.VMEM((GROUPS, per_dir, group, CHUNK), jnp.bfloat16),
            pltpu.SemaphoreType.DMA((4 + PARTS,)),
            pltpu.SemaphoreType.DMA((GROUPS, 2, per_dir)),
            pltpu.SemaphoreType.DMA((GROUPS, 2, per_dir)),
            pltpu.SemaphoreType.DMA((GROUPS, per_dir)),
            pltpu.SemaphoreType.DMA((GROUPS, per_dir)),
            pltpu.SemaphoreType.DMA((GROUPS, per_dir)),
        ],
        compiler_params=pltpu.CompilerParams(collective_id=0, has_side_effects=True),
    )(
        blocks.reshape(nnz, order, order),
        pattern.reshape(1, nnz),
        local_src.reshape(rows, width),
        owner,
    )
    return result.reshape(1, 1, nbatch, nsource, width)


def solution(mesh):
    return jax.shard_map(
        functools.partial(body, mesh.shape["gx"], mesh.shape["gy"]),
        mesh=mesh,
        in_specs=(
            P("gx", "gy", None, None, None),
            P("gx", "gy", None),
            P("gx", "gy", None, None, None),
            P(),
        ),
        out_specs=P("gx", "gy", None, None, None),
        check_vma=False,
    )
```

```python
import functools

import jax
import jax.numpy as jnp
from jax import lax
from jax.experimental import pallas as pl
from jax.experimental.pallas import tpu as pltpu
from jax.sharding import PartitionSpec as P

MESH = pl.DeviceIdType.MESH
GROUPS = 2
CHUNK = 256
PARTS = 4
UNROLL = 16
HEAD = 2
LEFT, BOTTOM = 0, 1


def kernel(
    dims,
    blocks_hbm,
    pattern_hbm,
    src_hbm,
    owner_hbm,
    out_ref,
    blk,
    pat_v,
    own_v,
    src_v,
    inv_v,
    inv_s,
    acc,
    inbuf,
    outbuf,
    relay,
    load_sem,
    send_sem,
    recv_sem,
    relay_send,
    relay_recv,
    onward_sem,
):
    nx, ny, nnz, order, rows, width = dims
    trace = width // 2
    nblk = width // order
    group = rows // GROUPS
    per_dir = trace // CHUNK
    sub = CHUNK // order
    me_x = lax.axis_index("gx")
    me_y = lax.axis_index("gy")
    has = (me_x > 0, me_y > 0)
    sends = (me_x < nx - 1, me_y < ny - 1)
    before = ((me_x - 1, me_y), (me_x, me_y - 1))
    after = ((me_x + 1, me_y), (me_x, me_y + 1))

    relayed = nx > 1 and ny > 1
    origin = jnp.logical_and(me_x == 0, me_y == 0)
    helper = jnp.logical_and(me_x == 1, me_y == 0)
    above_origin = jnp.logical_and(me_x == 0, me_y == 1)
    if relayed:
        before_y = (jnp.where(above_origin, 1, me_x), me_y - 1)
        before = (before[0], before_y)

    barrier = pltpu.get_barrier_semaphore()
    for d in range(2):

        @pl.when(has[d])
        def _():
            pl.semaphore_signal(barrier, inc=1, device_id=before[d], device_id_type=MESH)

    pat_copy = pltpu.make_async_copy(pattern_hbm, pat_v, load_sem.at[0])
    own_copy = pltpu.make_async_copy(owner_hbm, own_v, load_sem.at[1])
    src_copy = pltpu.make_async_copy(src_hbm, src_v, load_sem.at[2])
    pat_copy.start()
    own_copy.start()
    src_copy.start()
    step = nnz // PARTS
    blk_copies = [
        pltpu.make_async_copy(
            blocks_hbm.at[pl.ds(p * step, step)],
            blk.at[pl.ds(p * step, step)],
            load_sem.at[3 + p],
        )
        for p in range(PARTS)
    ]
    for copy in blk_copies:
        copy.start()
    blk[nnz] = jnp.zeros((order, order), blk.dtype)

    any_input = jnp.logical_or(has[0], has[1])
    inv_copy = pltpu.make_async_copy(inv_v, inv_s, load_sem.at[3 + PARTS])

    @pl.when(any_input)
    def _():
        pat_copy.wait()
        pat_t = jnp.transpose(jnp.broadcast_to(pat_v[...], (nnz, nnz)))
        lane = lax.broadcasted_iota(jnp.int32, (nnz, nnz), 1)
        which = lax.broadcasted_iota(jnp.int32, (nnz, nnz), 0)
        for h in range(nblk * nblk // nnz):
            hit = jnp.where(pat_t == lane + h * nnz, which, nnz)
            inv_v[h : h + 1, :] = jnp.min(hit, axis=0, keepdims=True)
        inv_copy.start()

    own_copy.wait()
    src_copy.wait()
    cell_id = me_x * ny + me_y
    nbatch, nsource = own_v.shape
    eye = lax.broadcasted_iota(jnp.int32, (nsource, nsource), 0) == lax.broadcasted_iota(
        jnp.int32, (nsource, nsource), 1
    )
    for b in range(nbatch):
        mine = (own_v[b : b + 1, :] == cell_id).astype(jnp.float32)
        mask = jnp.sum(jnp.where(eye, mine, 0.0), axis=1, keepdims=True)
        span = pl.ds(b * nsource, nsource)
        acc[span, :] = src_v[span, :].astype(jnp.float32) * mask

    @pl.when(jnp.logical_and(any_input, jnp.logical_not(helper)))
    def _():
        for p, copy in enumerate(blk_copies):
            copy.wait()

            def turn(i, carry):
                for u in range(UNROLL):
                    at = p * step + i * UNROLL + u
                    blk[at] = jnp.transpose(blk[at])
                return carry

            lax.fori_loop(0, step // UNROLL, turn, 0)

    wanted = sum(s.astype(jnp.int32) for s in sends)
    if relayed:
        wanted = wanted + helper.astype(jnp.int32) - origin.astype(jnp.int32)

    @pl.when(wanted > 0)
    def _():
        pl.semaphore_wait(barrier, wanted)

    def transfer(g, d, c):
        return pltpu.make_async_remote_copy(
            src_ref=outbuf.at[g, d, c],
            dst_ref=inbuf.at[g, d, c],
            send_sem=send_sem.at[g, d, c],
            recv_sem=recv_sem.at[g, d, c],
            device_id=after[d],
            device_id_type=MESH,
        )

    def weights(o, k):
        rows_of = []
        for b in range(sub):
            parts = []
            for a in range(sub):
                f = (o * sub + a) * nblk + k * sub + b
                parts.append(blk[inv_s[f // nnz, f % nnz]])
            rows_of.append(jnp.concatenate(parts, axis=1))
        return jnp.concatenate(rows_of, axis=0)

    def as_stored(o, k):
        rows_of = []
        for a in range(sub):
            f = (o * sub + a) * nblk + k * sub
            parts = [blk[inv_s[(f + b) // nnz, (f + b) % nnz]] for b in range(sub)]
            rows_of.append(jnp.concatenate(parts, axis=1))
        return jnp.concatenate(rows_of, axis=0)

    def product(g, d, c, outs):
        wide = [weights(o, d * per_dir + c) for o in outs]
        return jnp.dot(
            inbuf[g, d, c],
            jnp.concatenate(wide, axis=1),
            preferred_element_type=jnp.float32,
        )

    def whole(d, c):
        return jnp.concatenate([inbuf[g, d, c] for g in range(GROUPS)], axis=0)

    def whole_product(d, c, outs):
        wide = [weights(o, d * per_dir + c) for o in outs]
        return jnp.dot(
            whole(d, c), jnp.concatenate(wide, axis=1), preferred_element_type=jnp.float32
        )

    def stored_product(c, outs):
        tall = [as_stored(o, c) for o in outs]
        return lax.dot_general(
            whole(LEFT, c),
            jnp.concatenate(tall, axis=0),
            (((1,), (1,)), ((), ())),
            preferred_element_type=jnp.float32,
        )

    def handed(g, c):
        return pltpu.make_async_remote_copy(
            src_ref=outbuf.at[g, BOTTOM, c],
            dst_ref=relay.at[g, c],
            send_sem=relay_send.at[g, c],
            recv_sem=relay_recv.at[g, c],
            device_id=(me_x + 1, me_y),
            device_id_type=MESH,
        )

    def onward(g, c):
        return pltpu.make_async_remote_copy(
            src_ref=relay.at[g, c],
            dst_ref=inbuf.at[g, BOTTOM, c],
            send_sem=onward_sem.at[g, c],
            recv_sem=recv_sem.at[g, BOTTOM, c],
            device_id=(me_x - 1, me_y + 1),
            device_id_type=MESH,
        )

    def place(g, d, c):
        return (pl.ds(g * group, group), pl.ds((d * per_dir + c) * CHUNK, CHUNK))

    def store(g, d, c, value):
        result = value.astype(jnp.bfloat16)
        outbuf[g, d, c] = result
        out_ref[place(g, d, c)] = result

    def send(g, d, c):
        @pl.when(sends[d])
        def _():
            transfer(g, d, c).start()

    def emit(g, d, c, value):
        store(g, d, c, value)
        send(g, d, c)

    pairs = [((LEFT, c), (BOTTOM, c)) for c in range(per_dir)]
    sideways, upwards = (
        [((d, c), (d, c + 1)) for c in range(0, per_dir, 2)] for d in (LEFT, BOTTOM)
    )

    def number(pair):
        return tuple(d * per_dir + c for d, c in pair)

    ordered = [(d, c) for c in range(per_dir) for d in (BOTTOM, LEFT)]
    @pl.when(jnp.logical_not(any_input))
    def _():
        for g in range(GROUPS):
            for d, c in ordered:
                if relayed and d == BOTTOM:
                    store(g, d, c, acc[place(g, d, c)])
                    handed(g, c).start()
                else:
                    emit(g, d, c, acc[place(g, d, c)])
        pat_copy.wait()
        for copy in blk_copies:
            copy.wait()

    @pl.when(any_input)
    def _():
        if relayed:

            @pl.when(helper)
            def _():
                for g in range(GROUPS):
                    for c in range(per_dir):
                        handed(g, c).wait_recv()
                        onward(g, c).start()

        @pl.when(helper)
        def _():
            for copy in blk_copies:
                copy.wait()

        inv_copy.wait()


        def gather(g, d, c, outs):
            transfer(g, d, c).wait_recv()
            for pair in outs:
                both = product(g, d, c, number(pair))
                for n, (od, oc) in enumerate(pair):
                    at = place(g, od, oc)
                    acc[at] = acc[at] + both[:, n * CHUNK : (n + 1) * CHUNK]

        def finish(g, last, outs):
            for d, c in last:
                transfer(g, d, c).wait_recv()
            for pair in outs:
                both = sum(product(g, d, c, number(pair)) for d, c in last)
                for n, (od, oc) in enumerate(pair):
                    value = acc[place(g, od, oc)] + both[:, n * CHUNK : (n + 1) * CHUNK]
                    emit(g, od, oc, value)

        def split(dirs):
            early = [(d, c) for d in dirs[:-1] for c in range(per_dir)]
            early += [(dirs[-1], c) for c in range(HEAD)]
            return early, [(dirs[-1], c) for c in range(HEAD, per_dir)]

        def anywhere(dirs):
            early, last = split(dirs)
            for g in range(GROUPS):
                for d, c in early:
                    gather(g, d, c, pairs)
                finish(g, last, pairs)

        def top_row(dirs):
            early, last = split(dirs)
            early, last = early + last[:-1], last[-1:]
            for g in range(GROUPS):
                for d, c in early:
                    gather(g, d, c, sideways)
                finish(g, last, sideways)
            for pair in upwards:
                both = sum(whole_product(d, c, number(pair)) for d, c in early + last)
                for n, (od, oc) in enumerate(pair):
                    at = (slice(None), pl.ds((od * per_dir + oc) * CHUNK, CHUNK))
                    value = acc[at] + both[:, n * CHUNK : (n + 1) * CHUNK]
                    out_ref[at] = value.astype(jnp.bfloat16)

        def across(pair):
            return [
                (slice(None), pl.ds((od * per_dir + oc) * CHUNK, CHUNK)) for od, oc in pair
            ]

        def last_cell(dirs):
            early, last = split(dirs)
            early, last = early + last[:-1], last[-1:]
            for g in range(GROUPS):
                for d, c in early:
                    if d == dirs[0]:
                        gather(g, d, c, pairs)
            for d, c in early:
                if d != dirs[0]:
                    for g in range(GROUPS):
                        transfer(g, d, c).wait_recv()
                    for pair in pairs:
                        both = whole_product(d, c, number(pair))
                        for n, at in enumerate(across(pair)):
                            acc[at] = acc[at] + both[:, n * CHUNK : (n + 1) * CHUNK]
            for d, c in last:
                for g in range(GROUPS):
                    transfer(g, d, c).wait_recv()
            for pair in pairs:
                both = sum(whole_product(d, c, number(pair)) for d, c in last)
                for n, at in enumerate(across(pair)):
                    value = acc[at] + both[:, n * CHUNK : (n + 1) * CHUNK]
                    out_ref[at] = value.astype(jnp.bfloat16)

        top = jnp.logical_and(has[BOTTOM], jnp.logical_not(sends[BOTTOM]))
        end = jnp.logical_and(jnp.logical_and(top, has[LEFT]), jnp.logical_not(sends[LEFT]))
        below = jnp.logical_not(top)
        plans = (
            (below, (BOTTOM, LEFT), anywhere),
            (below, (LEFT,), anywhere),
            (below, (BOTTOM,), anywhere),
            (jnp.logical_and(top, jnp.logical_not(end)), (BOTTOM, LEFT), top_row),
            (top, (BOTTOM,), top_row),
            (end, (BOTTOM, LEFT), last_cell),
        )
        for where, dirs, plan in plans:
            here = [has[d] if d in dirs else jnp.logical_not(has[d]) for d in range(2)]
            here = jnp.logical_and(jnp.logical_and(here[0], here[1]), jnp.logical_not(helper))

            @pl.when(jnp.logical_and(here, where))
            def _():
                plan(dirs)

        @pl.when(helper)
        def _():
            for g in range(GROUPS):
                for c in range(per_dir):
                    transfer(g, LEFT, c).wait_recv()
            for pair in sideways + upwards:
                both = sum(stored_product(c, number(pair)) for c in range(per_dir))
                for g in range(GROUPS):
                    for n, (od, oc) in enumerate(pair):
                        part = both[g * group : (g + 1) * group, n * CHUNK : (n + 1) * CHUNK]
                        emit(g, od, oc, acc[place(g, od, oc)] + part)

    for g in range(GROUPS):
        for d in (LEFT, BOTTOM):
            for c in range(per_dir):
                if relayed and d == BOTTOM:

                    @pl.when(jnp.logical_and(sends[d], jnp.logical_not(origin)))
                    def _():
                        transfer(g, d, c).wait_send()

                    @pl.when(origin)
                    def _():
                        handed(g, c).wait_send()

                    @pl.when(helper)
                    def _():
                        onward(g, c).wait_send()

                else:

                    @pl.when(sends[d])
                    def _():
                        transfer(g, d, c).wait_send()


def body(nx, ny, blocks, pattern, local_src, owner):
    nnz, order = blocks.shape[2], blocks.shape[3]
    nbatch, nsource, width = local_src.shape[2:]
    rows = nbatch * nsource
    nblk = width // order
    per_dir = width // 2 // CHUNK
    group = rows // GROUPS
    dims = (nx, ny, nnz, order, rows, width)
    any_spec = pl.BlockSpec(memory_space=pl.ANY)
    result = pl.pallas_call(
        functools.partial(kernel, dims),
        name="sweep",
        out_shape=pltpu.VMEM((rows, width), jnp.bfloat16),
        in_specs=[any_spec] * 4,
        out_specs=pl.BlockSpec(memory_space=pltpu.VMEM),
        scratch_shapes=[
            pltpu.VMEM((nnz + 1, order, order), jnp.bfloat16),
            pltpu.VMEM((1, nnz), jnp.int32),
            pltpu.VMEM((nbatch, nsource), jnp.int32),
            pltpu.VMEM((rows, width), jnp.bfloat16),
            pltpu.VMEM((nblk * nblk // nnz, nnz), jnp.int32),
            pltpu.SMEM((nblk * nblk // nnz, nnz), jnp.int32),
            pltpu.VMEM((rows, width), jnp.float32),
            pltpu.VMEM((GROUPS, 2, per_dir, group, CHUNK), jnp.bfloat16),
            pltpu.VMEM((GROUPS, 2, per_dir, group, CHUNK), jnp.bfloat16),
            pltpu.VMEM((GROUPS, per_dir, group, CHUNK), jnp.bfloat16),
            pltpu.SemaphoreType.DMA((4 + PARTS,)),
            pltpu.SemaphoreType.DMA((GROUPS, 2, per_dir)),
            pltpu.SemaphoreType.DMA((GROUPS, 2, per_dir)),
            pltpu.SemaphoreType.DMA((GROUPS, per_dir)),
            pltpu.SemaphoreType.DMA((GROUPS, per_dir)),
            pltpu.SemaphoreType.DMA((GROUPS, per_dir)),
        ],
        compiler_params=pltpu.CompilerParams(collective_id=0, has_side_effects=True),
    )(
        blocks.reshape(nnz, order, order),
        pattern.reshape(1, nnz),
        local_src.reshape(rows, width),
        owner,
    )
    return result.reshape(1, 1, nbatch, nsource, width)


def solution(mesh):
    return jax.shard_map(
        functools.partial(body, mesh.shape["gx"], mesh.shape["gy"]),
        mesh=mesh,
        in_specs=(
            P("gx", "gy", None, None, None),
            P("gx", "gy", None),
            P("gx", "gy", None, None, None),
            P(),
        ),
        out_specs=P("gx", "gy", None, None, None),
        check_vma=False,
    )
```
